32 devices in a mesh: row: 16 (over z, y, x), col: 2 (over core).
Axes of the slice: x: 2, y: 2, z: 4, core: 2. Of those that a mesh axis runs over, the one named last changes fastest.
Arguments:
- matrix: float32 [4096, 4096], P('row', 'col'), may hold values from -15.625 to 15.625
Outputs:
- r_top: float32 [512, 4096], P(None, 'col')
- basis: float32 [4096, 512], P('row')
The draws below stay inside these ranges and needn't reach their ends.
All inputs are finite; a program needn't handle non-finite values.
Results may differ from the reference program's by a relative error of at most 0.0003.
Values sent between devices are 32-bit elements; how exact they have to be, the bound alone decides.
A program may use at most 64 MiB of HBM per device.

```python
import math
import jax
import jax.numpy as jnp
from jax import lax

PANEL = 256
NCOLS = 4096
ROWS = 4096


def mixing(key, width, spread):
    keys = jax.random.split(key, 2)
    left, unused_left = jnp.linalg.qr(jax.random.normal(keys[0], (width, width), jnp.float32))
    right, unused_right = jnp.linalg.qr(jax.random.normal(keys[1], (width, width), jnp.float32))
    levels = jnp.exp(-math.log(spread) * jnp.arange(width, dtype=jnp.float32) / (width - 1))
    mixed = jnp.dot(left * levels[None, :], right.T, precision=lax.Precision.HIGHEST)
    return mixed / jnp.sqrt(jnp.sum(mixed * mixed, axis=0, keepdims=True))


def draw_matrix(key, part):
    base = jax.random.fold_in(key, 11)
    keys = jax.random.split(base, 11)
    noise = jnp.clip(jax.random.normal(keys[0], (ROWS, NCOLS), jnp.float32), -6.0, 6.0)
    shared = jnp.clip(jax.random.normal(keys[3], (ROWS, 1), jnp.float32), -3.0, 3.0)
    weights = jnp.clip(jax.random.normal(keys[4], (1, NCOLS), jnp.float32), -3.0, 3.0)
    spread = 4.0
    row_span = math.log(2.0)
    ramp_span = math.log(3.0)
    common = 0.0 * shared * weights
    first = jnp.dot(noise[:, :PANEL], mixing(keys[5], PANEL, spread), precision=lax.Precision.HIGHEST)
    second = jnp.dot(noise[:, PANEL:2 * PANEL], mixing(keys[6], PANEL, spread), precision=lax.Precision.HIGHEST)
    panels = jnp.clip(jnp.concatenate([first, second], axis=1), -8.0, 8.0)
    values = jnp.concatenate([panels, noise[:, 2 * PANEL:]], axis=1) + common
    ramp = jnp.exp(ramp_span * jnp.arange(ROWS, dtype=jnp.float32) / ROWS)
    row_scale = ramp * jnp.exp(jax.random.uniform(keys[1], (ROWS,), jnp.float32, 0.0, row_span))
    col_scale = jnp.exp(jax.random.uniform(keys[2], (NCOLS,), jnp.float32, 0.0, math.log(3.0)))
    values = values * row_scale[:, None] * col_scale[None, :] / math.sqrt(ROWS)
    bound = 1000.0 / math.sqrt(ROWS)
    row_high = jax.random.randint(keys[7], (), 0, ROWS)
    row_low = (row_high + jax.random.randint(keys[8], (), 1, ROWS)) % ROWS
    col_high = jax.random.randint(keys[9], (), 2 * PANEL, NCOLS)
    col_low = jax.random.randint(keys[10], (), 2 * PANEL, NCOLS)
    values = values.at[row_high, col_high].set(bound)
    values = values.at[row_low, col_low].set(-bound)
    return values.astype(jnp.float32)


def setup_inputs(seed: int = 0) -> dict:
    key_list = jax.random.split(jax.random.key(seed), 2)
    matrix = draw_matrix(jax.random.fold_in(key_list[1], 71), 0)
    return dict(matrix=matrix)


def signed_qr(panel):
    left, right = jnp.linalg.qr(panel)
    signs = jnp.sign(jnp.diagonal(right))
    return (left * signs[None, :], right * signs[:, None])

def reference(matrix):
    highest = lax.Precision.HIGHEST
    panel_cols = PANEL
    q_first, r_first = signed_qr(matrix[:, :panel_cols])
    z_first = jnp.dot(q_first.T, matrix[:, panel_cols:], precision=highest)
    second = matrix[:, panel_cols:2 * panel_cols] - jnp.dot(q_first, z_first[:, :panel_cols], precision=highest)
    q_second, r_second = signed_qr(second)
    cross = jnp.dot(q_second.T, q_first, precision=highest)
    z_second = jnp.dot(q_second.T, matrix[:, 2 * panel_cols:], precision=highest) - jnp.dot(cross, z_first[:, panel_cols:], precision=highest)
    zeros = jnp.zeros((panel_cols, panel_cols), jnp.float32)
    top = jnp.concatenate([jnp.concatenate([r_first, z_first], axis=1), jnp.concatenate([zeros, r_second, z_second], axis=1)], axis=0)
    basis = jnp.concatenate([q_first, q_second], axis=1) * math.sqrt(ROWS)
    return (top, basis)
```

```python
import functools
import math

import jax
import jax.numpy as jnp
from jax import lax
from jax.experimental import pallas as pl
from jax.experimental.pallas import tpu as pltpu
from jax.sharding import PartitionSpec as P

PANEL = 256
WIDE = 2 * PANEL
LANE = 128
SUB = 8
HIGHEST = lax.Precision.HIGHEST
MESH = pl.DeviceIdType.MESH


def dot(a, b, ca=1, cb=0):
    return lax.dot_general(
        a, b, (((ca,), (cb,)), ((), ())), precision=HIGHEST, preferred_element_type=jnp.float32
    )


def row_chunks(rows):
    units = rows // SUB
    sizes = [units // 3 + (1 if i < units % 3 else 0) for i in range(3)]
    out, at = [], 0
    for size in sizes:
        if size:
            out.append((at * SUB, size * SUB))
            at += size
    return out


class AllReduce:
    def __init__(self, src, recv, dst, sems, n_row, me, col):
        self.src, self.recv, self.dst = src, recv, dst
        self.sems = sems
        self.n = n_row
        self.bits = n_row.bit_length() - 1
        self.col = col
        self.me = me
        self.chunks = []
        spin = max(self.bits - 1, 1)
        for c, (ro, rn) in enumerate(row_chunks(src.shape[1])):
            order = [(c + t) % spin for t in range(spin)] + list(range(spin, self.bits))
            starts = [0]
            mine = []
            for s, b in enumerate(order):
                bit = (me // (1 << b)) % 2
                mine.append(bit)
                starts.append(starts[-1] + bit * (n_row >> (s + 1)))
            self.chunks.append((c, ro, rn, order, starts, mine))

    def partner(self, b, bit):
        return self.me + (1 << b) * (1 - 2 * bit)

    def rs_copy(self, s, chunk):
        c, ro, rn, order, starts, mine = chunk
        half = self.n >> (s + 1)
        off = self.n - (self.n >> s)
        bit = mine[s]
        send = starts[s] + (1 - bit) * half
        return pltpu.make_async_remote_copy(
            src_ref=self.src.at[pl.ds(send, half), pl.ds(ro, rn), :],
            dst_ref=self.recv.at[pl.ds(off, half), pl.ds(ro, rn), :],
            send_sem=self.sems.at[0, s, c],
            recv_sem=self.sems.at[1, s, c],
            device_id=(self.partner(order[s], bit), self.col),
            device_id_type=MESH,
        )

    def rs_start(self, s):
        for chunk in self.chunks:
            self.rs_copy(s, chunk).start()

    def rs_finish(self, s):
        half = self.n >> (s + 1)
        off = self.n - (self.n >> s)
        last = s == self.bits - 1
        for chunk in self.chunks:
            c, ro, rn, order, starts, mine = chunk
            self.rs_copy(s, chunk).wait()
            keep = starts[s + 1]
            into = self.dst if last else self.src

            def add(i, carry, ro=ro, rn=rn, keep=keep, into=into):
                rows = pl.ds(ro, rn)
                into[keep + i, rows, :] = self.src[keep + i, rows, :] + self.recv[off + i, rows, :]
                return carry

            lax.fori_loop(0, half, add, 0)
            if not last:
                self.rs_copy(s + 1, chunk).start()
            else:
                self.ag_copy(s, chunk).start()

    def ag_copy(self, s, chunk):
        c, ro, rn, order, starts, mine = chunk
        half = self.n >> (s + 1)
        bit = mine[s]
        region = self.dst.at[pl.ds(starts[s + 1], half), pl.ds(ro, rn), :]
        return pltpu.make_async_remote_copy(
            src_ref=region,
            dst_ref=region,
            send_sem=self.sems.at[2, s, c],
            recv_sem=self.sems.at[3, s, c],
            device_id=(self.partner(order[s], bit), self.col),
            device_id_type=MESH,
        )

    def ag_finish(self, s):
        for chunk in self.chunks:
            self.ag_copy(s, chunk).wait()
            if s > 0:
                self.ag_copy(s - 1, chunk).start()

    def steps(self):
        out = [functools.partial(self.rs_finish, s) for s in range(self.bits)]
        out += [functools.partial(self.ag_finish, s) for s in reversed(range(self.bits))]
        return out


def factor_panels(t_ref, k, lo, hi):
    base = k * LANE
    size = t_ref.shape[0]
    lane = lax.broadcasted_iota(jnp.int32, (SUB, LANE), 1)
    sub = lax.broadcasted_iota(jnp.int32, (SUB, LANE), 0)
    wide_lane = lax.broadcasted_iota(jnp.int32, (SUB, size), 1)
    wide_sub = lax.broadcasted_iota(jnp.int32, (SUB, size), 0)

    def one(p, carry):
        r0 = pl.multiple_of(base + p * SUB, SUB)
        pan = t_ref[pl.ds(r0, SUB), :]
        x = pltpu.roll(pan[:, base : base + LANE], (LANE - p * SUB) % LANE, 1)
        for j in range(SUB - 1):
            col = x[:, j : j + 1]
            m = jnp.where(sub[:, :1] > j, col / col[j : j + 1, :], 0.0)
            row = jnp.where(lane[:1] == j, 1.0, x[j : j + 1, :])
            x = jnp.where((lane == j) & (sub > j), 0.0, x) - m * row
        diag = jnp.sum(jnp.where(lane == sub, x, 0.0), axis=1, keepdims=True)
        scale = 1.0 / jnp.sqrt(diag)
        inv = jnp.where(lane == sub, 1.0, jnp.where(lane < sub, x, 0.0)) * scale
        rel = wide_lane - r0
        inside = (rel >= 0) & (rel < SUB)
        pan = jnp.where(inside, jnp.where(rel == wide_sub, 1.0, 0.0), pan)
        top = inv[:, 0:1] * pan[0:1, :]
        for j in range(1, SUB):
            top = top + inv[:, j : j + 1] * pan[j : j + 1, :]
        w = jnp.where(rel >= SUB, top, 0.0)
        upd = dot(w[:, base:], top, 0, 0)
        rel_all = lax.broadcasted_iota(jnp.int32, (size - base, size), 1) - r0
        clear = (rel_all >= 0) & (rel_all < SUB)
        t_ref[base:, :] = jnp.where(clear, 0.0, t_ref[base:, :]) - upd
        t_ref[pl.ds(r0, SUB), :] = top
        return carry

    lax.fori_loop(lo, hi, one, 0)


def kernel(n_row, n_col, scale, a_ref, top_ref, basis_ref, a12, a12t, p, p_in, q, g, g_in, gq, t,
           p_sems, g_sems, bsend, brecv):
    me = lax.axis_index("row")
    col = lax.axis_index("col")
    bits = n_row.bit_length() - 1
    blocks = a_ref.shape[1] // LANE
    gblocks = WIDE // LANE
    p_split = p.shape[0] // blocks
    g_split = g.shape[0] // gblocks

    barrier = pltpu.get_barrier_semaphore()
    for b in range(bits):
        bit = (me // (1 << b)) % 2
        pl.semaphore_signal(
            barrier, inc=1, device_id=(me + (1 << b) * (1 - 2 * bit), col), device_id_type=MESH
        )
    for c in range(1, n_col):
        pl.semaphore_signal(barrier, inc=1, device_id=(me, (col + c) % n_col), device_id_type=MESH)
    pl.semaphore_wait(barrier, bits + n_col - 1)

    def panel_copy(c):
        return pltpu.make_async_remote_copy(
            src_ref=a_ref.at[:, pl.ds(0, WIDE)],
            dst_ref=a12,
            send_sem=bsend.at[c],
            recv_sem=brecv.at[0],
            device_id=(me, c),
            device_id_type=MESH,
        )

    @pl.when(col == 0)
    def _():
        for c in range(1, n_col):
            panel_copy(c).start()
        a12[...] = a_ref[:, :WIDE]
        for c in range(1, n_col):
            panel_copy(c).wait_send()

    @pl.when(col != 0)
    def _():
        panel_copy(0).wait_recv()

    a12t[...] = a12[...].T

    def fill(dst, src, split):
        pair = 2 * LANE

        def one(i, carry):
            val = dot(a12t[...], src[:, pl.ds(pl.multiple_of(i * pair, pair), pair)])
            for h in range(2):
                part = val[:, h * LANE : (h + 1) * LANE]
                dst[pl.ds((2 * i + h) * split, split)] = part.reshape(split, WIDE // split, LANE)
            return carry

        lax.fori_loop(0, src.shape[1] // pair, one, 0)

    fill(g, a12, g_split)
    g_red = AllReduce(g, g_in, gq, g_sems, n_row, me, col)
    g_red.rs_start(0)
    fill(p, a_ref, p_split)
    for step in g_red.steps():
        step()
    p_red = AllReduce(p, p_in, q, p_sems, n_row, me, col)
    p_red.rs_start(0)
    for b in range(gblocks):
        t[:, b * LANE : (b + 1) * LANE] = gq[b * g_split : (b + 1) * g_split].reshape(WIDE, LANE)

    per = LANE // SUB
    units = [(k, lo, lo + per // 2) for k in range(gblocks) for lo in (0, per // 2)]
    steps = p_red.steps()
    done = 0
    for i, step in enumerate(steps):
        upto = len(units) * (i + 1) // len(steps)
        for unit in units[done:upto]:
            factor_panels(t, *unit)
        done = upto
        step()

    rows = lax.broadcasted_iota(jnp.int32, (WIDE, WIDE), 0)
    cols = lax.broadcasted_iota(jnp.int32, (WIDE, WIDE), 1)
    t[...] = jnp.where(cols <= rows, t[...], 0.0)
    basis_ref[...] = dot(a12[...], t[...], 1, 1) * scale

    def finish(i, carry):
        pair = 2 * LANE
        parts = [
            q[pl.ds((2 * i + h) * p_split, p_split)].reshape(WIDE, LANE) for h in range(2)
        ]
        val = dot(t[...], jnp.concatenate(parts, axis=1))
        r = lax.broadcasted_iota(jnp.int32, (WIDE, pair), 0)
        c = lax.broadcasted_iota(jnp.int32, (WIDE, pair), 1) + col * a_ref.shape[1] + i * pair
        top_ref[:, pl.ds(pl.multiple_of(i * pair, pair), pair)] = jnp.where(c >= r, val, 0.0)
        return carry

    lax.fori_loop(0, blocks // 2, finish, 0)


def body(n_row, n_col, matrix):
    height, width = matrix.shape
    scale = math.sqrt(height * n_row)
    bits = n_row.bit_length() - 1
    p_shape = (n_row, (width // LANE) * WIDE // n_row, LANE)
    g_shape = (n_row, (WIDE // LANE) * WIDE // n_row, LANE)
    f32 = jnp.float32
    vmem = pl.BlockSpec(memory_space=pltpu.VMEM)
    return pl.pallas_call(
        functools.partial(kernel, n_row, n_col, scale),
        out_shape=(
            jax.ShapeDtypeStruct((WIDE, width), f32),
            jax.ShapeDtypeStruct((height, WIDE), f32),
        ),
        in_specs=[vmem],
        out_specs=(vmem, vmem),
        scratch_shapes=[
            pltpu.VMEM((height, WIDE), f32),
            pltpu.VMEM((WIDE, height), f32),
            pltpu.VMEM(p_shape, f32),
            pltpu.VMEM(p_shape, f32),
            pltpu.VMEM(p_shape, f32),
            pltpu.VMEM(g_shape, f32),
            pltpu.VMEM(g_shape, f32),
            pltpu.VMEM(g_shape, f32),
            pltpu.VMEM((WIDE, WIDE), f32),
            pltpu.SemaphoreType.DMA((4, bits, 3)),
            pltpu.SemaphoreType.DMA((4, bits, 3)),
            pltpu.SemaphoreType.DMA((n_col,)),
            pltpu.SemaphoreType.DMA((1,)),
        ],
        compiler_params=pltpu.CompilerParams(
            collective_id=0, has_side_effects=True, vmem_limit_bytes=60 * 1024 * 1024
        ),
    )(matrix)


def solution(mesh):
    return jax.shard_map(
        functools.partial(body, mesh.shape["row"], mesh.shape["col"]),
        mesh=mesh,
        in_specs=(P("row", "col"),),
        out_specs=(P(None, "col"), P("row", None)),
        check_vma=False,
    )
```

```python
import functools
import math

import jax
import jax.numpy as jnp
from jax import lax
from jax.experimental import pallas as pl
from jax.experimental.pallas import tpu as pltpu
from jax.sharding import PartitionSpec as P

PANEL = 256
WIDE = 2 * PANEL
LANE = 128
SUB = 8
P_CHUNKS = 6
HIGHEST = lax.Precision.HIGHEST
MESH = pl.DeviceIdType.MESH


def dot(a, b, ca=1, cb=0):
    return lax.dot_general(
        a, b, (((ca,), (cb,)), ((), ())), precision=HIGHEST, preferred_element_type=jnp.float32
    )


def row_chunks(rows, count):
    units = rows // SUB
    sizes = [units // count + (1 if i < units % count else 0) for i in range(count)]
    out, at = [], 0
    for size in sizes:
        if size:
            out.append((at * SUB, size * SUB))
            at += size
    return out


class AllReduce:
    def __init__(self, src, recv, dst, sems, n_row, me, col, count):
        self.src, self.recv, self.dst = src, recv, dst
        self.sems = sems
        self.n = n_row
        self.bits = n_row.bit_length() - 1
        self.col = col
        self.me = me
        self.chunks = []
        spin = max(self.bits - 1, 1)
        for c, (ro, rn) in enumerate(row_chunks(src.shape[1], count)):
            order = [(c + t) % spin for t in range(spin)] + list(range(spin, self.bits))
            starts = [0]
            mine = []
            for s, b in enumerate(order):
                bit = (me // (1 << b)) % 2
                mine.append(bit)
                starts.append(starts[-1] + bit * (n_row >> (s + 1)))
            self.chunks.append((c, ro, rn, order, starts, mine))

    def partner(self, b, bit):
        return self.me + (1 << b) * (1 - 2 * bit)

    def rs_copy(self, s, chunk):
        c, ro, rn, order, starts, mine = chunk
        half = self.n >> (s + 1)
        off = self.n - (self.n >> s)
        bit = mine[s]
        send = starts[s] + (1 - bit) * half
        return pltpu.make_async_remote_copy(
            src_ref=self.src.at[pl.ds(send, half), pl.ds(ro, rn), :],
            dst_ref=self.recv.at[pl.ds(off, half), pl.ds(ro, rn), :],
            send_sem=self.sems.at[0, s, c],
            recv_sem=self.sems.at[1, s, c],
            device_id=(self.partner(order[s], bit), self.col),
            device_id_type=MESH,
        )

    def rs_start(self, s):
        for chunk in self.chunks:
            self.rs_copy(s, chunk).start()

    def rs_finish(self, s, chunks):
        half = self.n >> (s + 1)
        off = self.n - (self.n >> s)
        last = s == self.bits - 1
        for chunk in chunks:
            c, ro, rn, order, starts, mine = chunk
            self.rs_copy(s, chunk).wait()
            keep = starts[s + 1]
            into = self.dst if last else self.src

            def add(i, carry, ro=ro, rn=rn, keep=keep, into=into):
                rows = pl.ds(ro, rn)
                into[keep + i, rows, :] = self.src[keep + i, rows, :] + self.recv[off + i, rows, :]
                return carry

            lax.fori_loop(0, half, add, 0)
            if not last:
                self.rs_copy(s + 1, chunk).start()
            else:
                self.ag_copy(s, chunk).start()

    def ag_copy(self, s, chunk):
        c, ro, rn, order, starts, mine = chunk
        half = self.n >> (s + 1)
        bit = mine[s]
        region = self.dst.at[pl.ds(starts[s + 1], half), pl.ds(ro, rn), :]
        return pltpu.make_async_remote_copy(
            src_ref=region,
            dst_ref=region,
            send_sem=self.sems.at[2, s, c],
            recv_sem=self.sems.at[3, s, c],
            device_id=(self.partner(order[s], bit), self.col),
            device_id_type=MESH,
        )

    def ag_finish(self, s, chunks):
        for chunk in chunks:
            self.ag_copy(s, chunk).wait()
            if s > 0:
                self.ag_copy(s - 1, chunk).start()

    def steps(self):
        groups = [self.chunks[i : i + 3] for i in range(0, len(self.chunks), 3)]
        out = []
        for s in range(self.bits):
            out += [functools.partial(self.rs_finish, s, group) for group in groups]
        for s in reversed(range(self.bits)):
            out += [functools.partial(self.ag_finish, s, group) for group in groups]
        return out


def split3(x):
    hi = x.astype(jnp.bfloat16).astype(jnp.float32)
    rest = x - hi
    mid = rest.astype(jnp.bfloat16).astype(jnp.float32)
    return hi, mid, rest - mid


def split2(x):
    hi = x.astype(jnp.bfloat16)
    return hi, (x - hi.astype(jnp.float32)).astype(jnp.bfloat16)


def dot3(a, b):
    def one(u, v):
        return jnp.dot(u, v, preferred_element_type=jnp.float32)

    return one(a[0], b[0]) + (one(a[0], b[1]) + one(a[1], b[0]))


def eliminate(x, lane, sub):
    d11 = d12 = d22 = None
    for a in range(0, SUB, 2):
        b = a + 1
        ca = jnp.broadcast_to(x[:, a : a + 1], x.shape)
        cb = jnp.broadcast_to(x[:, b : b + 1], x.shape)
        p11 = jnp.broadcast_to(ca[a : a + 1, :], x.shape)
        p12 = jnp.broadcast_to(cb[a : a + 1, :], x.shape)
        p22 = jnp.broadcast_to(cb[b : b + 1, :], x.shape)
        if a == 0:
            d11, d12, d22 = p11, p12, p22
        else:
            here = sub >= a
            d11 = jnp.where(here, p11, d11)
            d12 = jnp.where(here, p12, d12)
            d22 = jnp.where(here, p22, d22)
        if b == SUB - 1:
            break
        below = sub > b
        pair = (lane == a) | (lane == b)
        row_a = jnp.where(pair, jnp.where(lane == a, 1.0, 0.0), jnp.broadcast_to(x[a : a + 1, :], x.shape))
        row_b = jnp.where(pair, jnp.where(lane == b, 1.0, 0.0), jnp.broadcast_to(x[b : b + 1, :], x.shape))
        r = jnp.where(below, 1.0 / (p11 * p22 - p12 * p12), 0.0)
        num = (ca * p22 - cb * p12) * row_a + (cb * p11 - ca * p12) * row_b
        x = jnp.where(pair & below, 0.0, x) - num * r
    m = jnp.where(sub % 2 == 1, d12 / d11, 0.0)
    scale = lax.rsqrt(jnp.where(sub % 2 == 1, d22 - d12 * m, d11))
    y = jnp.where(lane == sub, 1.0, jnp.where(lane < sub - sub % 2, x, 0.0))
    return (y - m * pltpu.roll(y, 1, 0)) * scale


def factor_panels(t_ref, d_ref, k, lo, hi):
    base = k * LANE
    end = base + LANE
    size = t_ref.shape[0]
    lane = lax.broadcasted_iota(jnp.int32, (SUB, LANE), 1)
    sub = lax.broadcasted_iota(jnp.int32, (SUB, LANE), 0)
    full_lane = lax.broadcasted_iota(jnp.int32, (LANE, LANE), 1)
    full_sub = lax.broadcasted_iota(jnp.int32, (LANE, LANE), 0)
    if lo == 0:
        d_ref[...] = t_ref[base:end, base:end]

    def one(p, carry):
        r0 = pl.multiple_of(p * SUB, SUB)
        pan = d_ref[pl.ds(r0, SUB), :]
        inv = eliminate(pltpu.roll(pan, (LANE - r0) % LANE, 1), lane, sub)
        rel = lane - r0
        inside = (rel >= 0) & (rel < SUB)
        pan = jnp.where(inside, jnp.where(rel == sub, 1.0, 0.0), pan)
        terms = [inv[:, j : j + 1] * pan[j : j + 1, :] for j in range(SUB)]
        while len(terms) > 1:
            terms = [terms[i] + terms[i + 1] for i in range(0, len(terms), 2)]
        top = terms[0]
        m1, m2, m3 = split3(top)
        after = rel >= SUB
        w1, w2, w3 = (jnp.where(after, v, 0.0) for v in (m1, m2, m3))
        left = jnp.concatenate([w1, w1, w2, w1, w2, w3], axis=0).astype(jnp.bfloat16)
        right = jnp.concatenate([m1, m2, m1, m3, m2, m1], axis=0).astype(jnp.bfloat16)
        upd = lax.dot_general(
            left, right, (((0,), (0,)), ((), ())), preferred_element_type=jnp.float32
        )
        clear = (full_lane >= r0) & (full_lane < r0 + SUB)
        d_ref[...] = jnp.where(clear, 0.0, d_ref[...]) - upd
        d_ref[pl.ds(r0, SUB), :] = top
        return carry

    lax.fori_loop(lo, hi, one, 0)
    if hi * SUB == LANE:
        inv = jnp.where(full_lane <= full_sub, d_ref[...], 0.0)
        for c in range(size // LANE):
            at = slice(c * LANE, (c + 1) * LANE)
            if c != k:
                t_ref[base:end, at] = dot(inv, t_ref[base:end, at])
        t_ref[base:end, base:end] = inv
        if end < size:
            t_ref[end:, base:end] = jnp.zeros((size - end, LANE), jnp.float32)
            low = t_ref[base:end, end:].T
            t_ref[end:, :] = t_ref[end:, :] - dot(low, t_ref[base:end, :])


def kernel(n_row, n_col, scale, a_ref, top_ref, basis_ref, a12, a12t, p, p_in, q, g, g_in, gq, t, d,
           p_sems, g_sems, bsend, brecv):
    me = lax.axis_index("row")
    col = lax.axis_index("col")
    bits = n_row.bit_length() - 1
    blocks = a_ref.shape[1] // LANE
    gblocks = WIDE // LANE
    p_split = p.shape[0] // blocks
    g_split = g.shape[0] // gblocks

    barrier = pltpu.get_barrier_semaphore()
    for b in range(bits):
        bit = (me // (1 << b)) % 2
        pl.semaphore_signal(
            barrier, inc=1, device_id=(me + (1 << b) * (1 - 2 * bit), col), device_id_type=MESH
        )
    for c in range(1, n_col):
        pl.semaphore_signal(barrier, inc=1, device_id=(me, (col + c) % n_col), device_id_type=MESH)
    pl.semaphore_wait(barrier, bits + n_col - 1)

    def panel_copy(c):
        return pltpu.make_async_remote_copy(
            src_ref=a_ref.at[:, pl.ds(0, WIDE)],
            dst_ref=a12,
            send_sem=bsend.at[c],
            recv_sem=brecv.at[0],
            device_id=(me, c),
            device_id_type=MESH,
        )

    @pl.when(col == 0)
    def _():
        for c in range(1, n_col):
            panel_copy(c).start()
        a12[...] = a_ref[:, :WIDE]
        for c in range(1, n_col):
            panel_copy(c).wait_send()

    @pl.when(col != 0)
    def _():
        panel_copy(0).wait_recv()

    a12t[...] = a12[...].T

    def fill(dst, src, split, exact):
        pair = 2 * LANE
        left = a12t[...] if exact else split2(a12t[...])

        def one(i, carry):
            cols = src[:, pl.ds(pl.multiple_of(i * pair, pair), pair)]
            val = dot(left, cols) if exact else dot3(left, split2(cols))
            for h in range(2):
                part = val[:, h * LANE : (h + 1) * LANE]
                dst[pl.ds((2 * i + h) * split, split)] = part.reshape(split, WIDE // split, LANE)
            return carry

        lax.fori_loop(0, src.shape[1] // pair, one, 0)

    fill(g, a12, g_split, True)
    g_red = AllReduce(g, g_in, gq, g_sems, n_row, me, col, 3)
    g_red.rs_start(0)
    fill(p, a_ref, p_split, False)
    for step in g_red.steps():
        step()
    p_red = AllReduce(p, p_in, q, p_sems, n_row, me, col, P_CHUNKS)
    p_red.rs_start(0)
    for b in range(gblocks):
        t[:, b * LANE : (b + 1) * LANE] = gq[b * g_split : (b + 1) * g_split].reshape(WIDE, LANE)

    rows = lax.broadcasted_iota(jnp.int32, (WIDE, WIDE), 0)
    cols = lax.broadcasted_iota(jnp.int32, (WIDE, WIDE), 1)
    diag = jnp.where(cols == rows, t[...], 0.0)
    norm = lax.rsqrt(jnp.sum(diag, axis=0, keepdims=True))
    t[...] = t[...] * lax.rsqrt(jnp.sum(diag, axis=1, keepdims=True)) * norm

    per = LANE // SUB
    few = per // 4
    units = [(k, lo, lo + few) for k in range(gblocks) for lo in range(0, per, few)]
    steps = p_red.steps()
    done = 0
    for i, step in enumerate(steps):
        upto = len(units) * (i + 1) // len(steps)
        for unit in units[done:upto]:
            factor_panels(t, d, *unit)
        done = upto
        step()

    t[...] = jnp.where(cols <= rows, t[...] * norm, 0.0)
    basis_ref[...] = dot(a12[...], t[...], 1, 1) * scale

    inverse = split2(t[...])

    def finish(i, carry):
        pair = 2 * LANE
        parts = [
            q[pl.ds((2 * i + h) * p_split, p_split)].reshape(WIDE, LANE) for h in range(2)
        ]
        val = dot3(inverse, split2(jnp.concatenate(parts, axis=1)))
        r = lax.broadcasted_iota(jnp.int32, (WIDE, pair), 0)
        c = lax.broadcasted_iota(jnp.int32, (WIDE, pair), 1) + col * a_ref.shape[1] + i * pair
        top_ref[:, pl.ds(pl.multiple_of(i * pair, pair), pair)] = jnp.where(c >= r, val, 0.0)
        return carry

    lax.fori_loop(0, blocks // 2, finish, 0)


def body(n_row, n_col, matrix):
    height, width = matrix.shape
    scale = math.sqrt(height * n_row)
    bits = n_row.bit_length() - 1
    p_shape = (n_row, (width // LANE) * WIDE // n_row, LANE)
    g_shape = (n_row, (WIDE // LANE) * WIDE // n_row, LANE)
    f32 = jnp.float32
    vmem = pl.BlockSpec(memory_space=pltpu.VMEM)
    return pl.pallas_call(
        functools.partial(kernel, n_row, n_col, scale),
        out_shape=(
            jax.ShapeDtypeStruct((WIDE, width), f32),
            jax.ShapeDtypeStruct((height, WIDE), f32),
        ),
        in_specs=[vmem],
        out_specs=(vmem, vmem),
        scratch_shapes=[
            pltpu.VMEM((height, WIDE), f32),
            pltpu.VMEM((WIDE, height), f32),
            pltpu.VMEM(p_shape, f32),
            pltpu.VMEM(p_shape, f32),
            pltpu.VMEM(p_shape, f32),
            pltpu.VMEM(g_shape, f32),
            pltpu.VMEM(g_shape, f32),
            pltpu.VMEM(g_shape, f32),
            pltpu.VMEM((WIDE, WIDE), f32),
            pltpu.VMEM((LANE, LANE), f32),
            pltpu.SemaphoreType.DMA((4, bits, P_CHUNKS)),
            pltpu.SemaphoreType.DMA((4, bits, 3)),
            pltpu.SemaphoreType.DMA((n_col,)),
            pltpu.SemaphoreType.DMA((1,)),
        ],
        compiler_params=pltpu.CompilerParams(
            collective_id=0, has_side_effects=True, vmem_limit_bytes=60 * 1024 * 1024
        ),
    )(matrix)


def solution(mesh):
    return jax.shard_map(
        functools.partial(body, mesh.shape["row"], mesh.shape["col"]),
        mesh=mesh,
        in_specs=(P("row", "col"),),
        out_specs=(P(None, "col"), P("row", None)),
        check_vma=False,
    )
```

```python
import functools
import math

import jax
import jax.numpy as jnp
from jax import lax
from jax.experimental import pallas as pl
from jax.experimental.pallas import tpu as pltpu
from jax.sharding import PartitionSpec as P

PANEL = 256
WIDE = 2 * PANEL
LANE = 128
SUB = 8
P_CHUNKS = 6
HIGHEST = lax.Precision.HIGHEST
MESH = pl.DeviceIdType.MESH


def dot(a, b, ca=1, cb=0):
    return lax.dot_general(
        a, b, (((ca,), (cb,)), ((), ())), precision=HIGHEST, preferred_element_type=jnp.float32
    )


def row_chunks(rows, count):
    units = rows // SUB
    sizes = [units // count + (1 if i < units % count else 0) for i in range(count)]
    out, at = [], 0
    for size in sizes:
        if size:
            out.append((at * SUB, size * SUB))
            at += size
    return out


class AllReduce:
    def __init__(self, src, recv, dst, sems, n_row, me, col, count, base=0, height=None):
        self.src, self.recv, self.dst = src, recv, dst
        self.sems = sems
        self.n = n_row
        self.bits = n_row.bit_length() - 1
        self.col = col
        self.me = me
        self.chunks = []
        spin = max(self.bits - 1, 1)
        for c, (ro, rn) in enumerate(row_chunks(height or src.shape[1], count)):
            ro = pl.multiple_of(base + ro, SUB) if height else ro
            order = [(c + t) % spin for t in range(spin)] + list(range(spin, self.bits))
            starts = [0]
            mine = []
            for s, b in enumerate(order):
                bit = (me // (1 << b)) % 2
                mine.append(bit)
                starts.append(starts[-1] + bit * (n_row >> (s + 1)))
            self.chunks.append((c, ro, rn, order, starts, mine))

    def partner(self, b, bit):
        return self.me + (1 << b) * (1 - 2 * bit)

    def rs_copy(self, s, chunk):
        c, ro, rn, order, starts, mine = chunk
        half = self.n >> (s + 1)
        off = self.n - (self.n >> s)
        bit = mine[s]
        send = starts[s] + (1 - bit) * half
        return pltpu.make_async_remote_copy(
            src_ref=self.src.at[pl.ds(send, half), pl.ds(ro, rn), :],
            dst_ref=self.recv.at[pl.ds(off, half), pl.ds(ro, rn), :],
            send_sem=self.sems.at[0, s, c],
            recv_sem=self.sems.at[1, s, c],
            device_id=(self.partner(order[s], bit), self.col),
            device_id_type=MESH,
        )

    def rs_start(self, s):
        for chunk in self.chunks:
            self.rs_copy(s, chunk).start()

    def rs_finish(self, s, chunks):
        half = self.n >> (s + 1)
        off = self.n - (self.n >> s)
        last = s == self.bits - 1
        for chunk in chunks:
            c, ro, rn, order, starts, mine = chunk
            self.rs_copy(s, chunk).wait()
            keep = starts[s + 1]
            into = self.dst if last else self.src

            def add(i, carry, ro=ro, rn=rn, keep=keep, into=into):
                rows = pl.ds(ro, rn)
                into[keep + i, rows, :] = self.src[keep + i, rows, :] + self.recv[off + i, rows, :]
                return carry

            lax.fori_loop(0, half, add, 0)
            if not last:
                self.rs_copy(s + 1, chunk).start()
            else:
                self.ag_copy(s, chunk).start()

    def ag_copy(self, s, chunk):
        c, ro, rn, order, starts, mine = chunk
        half = self.n >> (s + 1)
        bit = mine[s]
        region = self.dst.at[pl.ds(starts[s + 1], half), pl.ds(ro, rn), :]
        return pltpu.make_async_remote_copy(
            src_ref=region,
            dst_ref=region,
            send_sem=self.sems.at[2, s, c],
            recv_sem=self.sems.at[3, s, c],
            device_id=(self.partner(order[s], bit), self.col),
            device_id_type=MESH,
        )

    def ag_finish(self, s, chunks):
        for chunk in chunks:
            self.ag_copy(s, chunk).wait()
            if s > 0:
                self.ag_copy(s - 1, chunk).start()

    def steps(self):
        groups = [self.chunks[i : i + 3] for i in range(0, len(self.chunks), 3)]
        out = []
        for s in range(self.bits):
            out += [functools.partial(self.rs_finish, s, group) for group in groups]
        for s in reversed(range(self.bits)):
            out += [functools.partial(self.ag_finish, s, group) for group in groups]
        return out


def split3(x):
    hi = x.astype(jnp.bfloat16).astype(jnp.float32)
    rest = x - hi
    mid = rest.astype(jnp.bfloat16).astype(jnp.float32)
    return hi, mid, rest - mid


def split2(x):
    hi = x.astype(jnp.bfloat16)
    return hi, (x - hi.astype(jnp.float32)).astype(jnp.bfloat16)


def dot3(a, b):
    def one(u, v):
        return jnp.dot(u, v, preferred_element_type=jnp.float32)

    return one(a[0], b[0]) + (one(a[0], b[1]) + one(a[1], b[0]))


def eliminate(x, lane, sub):
    d11 = d12 = d22 = None
    for a in range(0, SUB, 2):
        b = a + 1
        ca = jnp.broadcast_to(x[:, a : a + 1], x.shape)
        cb = jnp.broadcast_to(x[:, b : b + 1], x.shape)
        p11 = jnp.broadcast_to(ca[a : a + 1, :], x.shape)
        p12 = jnp.broadcast_to(cb[a : a + 1, :], x.shape)
        p22 = jnp.broadcast_to(cb[b : b + 1, :], x.shape)
        if a == 0:
            d11, d12, d22 = p11, p12, p22
        else:
            here = sub >= a
            d11 = jnp.where(here, p11, d11)
            d12 = jnp.where(here, p12, d12)
            d22 = jnp.where(here, p22, d22)
        if b == SUB - 1:
            break
        below = sub > b
        pair = (lane == a) | (lane == b)
        row_a = jnp.where(pair, jnp.where(lane == a, 1.0, 0.0), jnp.broadcast_to(x[a : a + 1, :], x.shape))
        row_b = jnp.where(pair, jnp.where(lane == b, 1.0, 0.0), jnp.broadcast_to(x[b : b + 1, :], x.shape))
        r = jnp.where(below, 1.0 / (p11 * p22 - p12 * p12), 0.0)
        num = (ca * p22 - cb * p12) * row_a + (cb * p11 - ca * p12) * row_b
        x = jnp.where(pair & below, 0.0, x) - num * r
    m = jnp.where(sub % 2 == 1, d12 / d11, 0.0)
    scale = lax.rsqrt(jnp.where(sub % 2 == 1, d22 - d12 * m, d11))
    y = jnp.where(lane == sub, 1.0, jnp.where(lane < sub - sub % 2, x, 0.0))
    return (y - m * pltpu.roll(y, 1, 0)) * scale


def factor_panels(t_ref, d_ref, k, lo, hi):
    base = k * LANE
    end = base + LANE
    size = t_ref.shape[0]
    lane = lax.broadcasted_iota(jnp.int32, (SUB, LANE), 1)
    sub = lax.broadcasted_iota(jnp.int32, (SUB, LANE), 0)
    full_lane = lax.broadcasted_iota(jnp.int32, (LANE, LANE), 1)
    full_sub = lax.broadcasted_iota(jnp.int32, (LANE, LANE), 0)
    if lo == 0:
        d_ref[...] = t_ref[base:end, base:end]

    def one(p, carry):
        r0 = pl.multiple_of(p * SUB, SUB)
        pan = d_ref[pl.ds(r0, SUB), :]
        inv = eliminate(pltpu.roll(pan, (LANE - r0) % LANE, 1), lane, sub)
        rel = lane - r0
        inside = (rel >= 0) & (rel < SUB)
        pan = jnp.where(inside, jnp.where(rel == sub, 1.0, 0.0), pan)
        terms = [inv[:, j : j + 1] * pan[j : j + 1, :] for j in range(SUB)]
        while len(terms) > 1:
            terms = [terms[i] + terms[i + 1] for i in range(0, len(terms), 2)]
        top = terms[0]
        m1, m2, m3 = split3(top)
        after = rel >= SUB
        w1, w2, w3 = (jnp.where(after, v, 0.0) for v in (m1, m2, m3))
        left = jnp.concatenate([w1, w1, w2, w1, w2, w3], axis=0).astype(jnp.bfloat16)
        right = jnp.concatenate([m1, m2, m1, m3, m2, m1], axis=0).astype(jnp.bfloat16)
        upd = lax.dot_general(
            left, right, (((0,), (0,)), ((), ())), preferred_element_type=jnp.float32
        )
        clear = (full_lane >= r0) & (full_lane < r0 + SUB)
        d_ref[...] = jnp.where(clear, 0.0, d_ref[...]) - upd
        d_ref[pl.ds(r0, SUB), :] = top
        return carry

    lax.fori_loop(lo, hi, one, 0)
    if hi * SUB == LANE:
        inv = jnp.where(full_lane <= full_sub, d_ref[...], 0.0)
        for c in range(size // LANE):
            at = slice(c * LANE, (c + 1) * LANE)
            if c != k:
                t_ref[base:end, at] = dot(inv, t_ref[base:end, at])
        t_ref[base:end, base:end] = inv
        if end < size:
            t_ref[end:, base:end] = jnp.zeros((size - end, LANE), jnp.float32)
            low = t_ref[base:end, end:].T
            t_ref[end:, :] = t_ref[end:, :] - dot(low, t_ref[base:end, :])


def kernel(n_row, n_col, scale, a_ref, top_ref, basis_ref, a12, a12t, p, p_in, q, g, g_in, gq, t, d,
           p_sems, g_sems, bsend, brecv, xsend, xrecv):
    me = lax.axis_index("row")
    col = lax.axis_index("col")
    bits = n_row.bit_length() - 1
    blocks = a_ref.shape[1] // LANE
    gblocks = WIDE // LANE
    p_split = p.shape[0] // blocks
    g_split = g.shape[0] // gblocks

    barrier = pltpu.get_barrier_semaphore()
    for b in range(bits):
        bit = (me // (1 << b)) % 2
        pl.semaphore_signal(
            barrier, inc=1, device_id=(me + (1 << b) * (1 - 2 * bit), col), device_id_type=MESH
        )
    for c in range(1, n_col):
        pl.semaphore_signal(barrier, inc=1, device_id=(me, (col + c) % n_col), device_id_type=MESH)
    pl.semaphore_wait(barrier, bits + n_col - 1)

    def panel_copy(c):
        return pltpu.make_async_remote_copy(
            src_ref=a_ref.at[:, pl.ds(0, WIDE)],
            dst_ref=a12,
            send_sem=bsend.at[c],
            recv_sem=brecv.at[0],
            device_id=(me, c),
            device_id_type=MESH,
        )

    @pl.when(col == 0)
    def _():
        for c in range(1, n_col):
            panel_copy(c).start()
        a12[...] = a_ref[:, :WIDE]
        for c in range(1, n_col):
            panel_copy(c).wait_send()

    @pl.when(col != 0)
    def _():
        panel_copy(0).wait_recv()

    a12t[...] = a12[...].T

    def fill(dst, src, split, exact):
        pair = 2 * LANE
        left = a12t[...] if exact else split2(a12t[...])

        def one(i, carry):
            cols = src[:, pl.ds(pl.multiple_of(i * pair, pair), pair)]
            val = dot(left, cols) if exact else dot3(left, split2(cols))
            for h in range(2):
                part = val[:, h * LANE : (h + 1) * LANE]
                dst[pl.ds((2 * i + h) * split, split)] = part.reshape(split, WIDE // split, LANE)
            return carry

        lax.fori_loop(0, src.shape[1] // pair, one, 0)

    fill(g, a12, g_split, True)
    shared = (g.shape[1] // SUB) % n_col == 0 and n_col > 1
    g_high = g.shape[1] // n_col if shared else None
    g_base = col * g_high if shared else 0
    g_red = AllReduce(g, g_in, gq, g_sems, n_row, me, col, 3, g_base, g_high)
    g_red.rs_start(0)
    fill(p, a_ref, p_split, False)
    for step in g_red.steps():
        step()
    if shared:
        part = gq.at[:, pl.ds(pl.multiple_of(g_base, SUB), g_high), :]
        swaps = [
            pltpu.make_async_remote_copy(
                src_ref=part,
                dst_ref=part,
                send_sem=xsend.at[c],
                recv_sem=xrecv.at[c],
                device_id=(me, (col + c) % n_col),
                device_id_type=MESH,
            )
            for c in range(1, n_col)
        ]
        for swap in swaps:
            swap.start()
    p_red = AllReduce(p, p_in, q, p_sems, n_row, me, col, P_CHUNKS)
    p_red.rs_start(0)
    if shared:
        for swap in swaps:
            swap.wait()
    for b in range(gblocks):
        t[:, b * LANE : (b + 1) * LANE] = gq[b * g_split : (b + 1) * g_split].reshape(WIDE, LANE)

    rows = lax.broadcasted_iota(jnp.int32, (WIDE, WIDE), 0)
    cols = lax.broadcasted_iota(jnp.int32, (WIDE, WIDE), 1)
    diag = jnp.where(cols == rows, t[...], 0.0)
    norm = lax.rsqrt(jnp.sum(diag, axis=0, keepdims=True))
    t[...] = t[...] * lax.rsqrt(jnp.sum(diag, axis=1, keepdims=True)) * norm

    per = LANE // SUB
    few = per // 4
    units = [(k, lo, lo + few) for k in range(gblocks) for lo in range(0, per, few)]
    steps = p_red.steps()
    done = 0
    for i, step in enumerate(steps):
        upto = len(units) * (i + 1) // len(steps)
        for unit in units[done:upto]:
            factor_panels(t, d, *unit)
        done = upto
        step()

    t[...] = jnp.where(cols <= rows, t[...] * norm, 0.0)
    basis_ref[...] = dot(a12[...], t[...], 1, 1) * scale

    inverse = split2(t[...])

    def finish(i, carry):
        pair = 2 * LANE
        parts = [
            q[pl.ds((2 * i + h) * p_split, p_split)].reshape(WIDE, LANE) for h in range(2)
        ]
        val = dot3(inverse, split2(jnp.concatenate(parts, axis=1)))
        r = lax.broadcasted_iota(jnp.int32, (WIDE, pair), 0)
        c = lax.broadcasted_iota(jnp.int32, (WIDE, pair), 1) + col * a_ref.shape[1] + i * pair
        top_ref[:, pl.ds(pl.multiple_of(i * pair, pair), pair)] = jnp.where(c >= r, val, 0.0)
        return carry

    lax.fori_loop(0, blocks // 2, finish, 0)


def body(n_row, n_col, matrix):
    height, width = matrix.shape
    scale = math.sqrt(height * n_row)
    bits = n_row.bit_length() - 1
    p_shape = (n_row, (width // LANE) * WIDE // n_row, LANE)
    g_shape = (n_row, (WIDE // LANE) * WIDE // n_row, LANE)
    f32 = jnp.float32
    vmem = pl.BlockSpec(memory_space=pltpu.VMEM)
    return pl.pallas_call(
        functools.partial(kernel, n_row, n_col, scale),
        out_shape=(
            jax.ShapeDtypeStruct((WIDE, width), f32),
            jax.ShapeDtypeStruct((height, WIDE), f32),
        ),
        in_specs=[vmem],
        out_specs=(vmem, vmem),
        scratch_shapes=[
            pltpu.VMEM((height, WIDE), f32),
            pltpu.VMEM((WIDE, height), f32),
            pltpu.VMEM(p_shape, f32),
            pltpu.VMEM(p_shape, f32),
            pltpu.VMEM(p_shape, f32),
            pltpu.VMEM(g_shape, f32),
            pltpu.VMEM(g_shape, f32),
            pltpu.VMEM(g_shape, f32),
            pltpu.VMEM((WIDE, WIDE), f32),
            pltpu.VMEM((LANE, LANE), f32),
            pltpu.SemaphoreType.DMA((4, bits, P_CHUNKS)),
            pltpu.SemaphoreType.DMA((4, bits, 3)),
            pltpu.SemaphoreType.DMA((n_col,)),
            pltpu.SemaphoreType.DMA((1,)),
            pltpu.SemaphoreType.DMA((n_col,)),
            pltpu.SemaphoreType.DMA((n_col,)),
        ],
        compiler_params=pltpu.CompilerParams(
            collective_id=0, has_side_effects=True, vmem_limit_bytes=60 * 1024 * 1024
        ),
    )(matrix)


def solution(mesh):
    return jax.shard_map(
        functools.partial(body, mesh.shape["row"], mesh.shape["col"]),
        mesh=mesh,
        in_specs=(P("row", "col"),),
        out_specs=(P(None, "col"), P("row", None)),
        check_vma=False,
    )
```

```python
import functools
import math

import jax
import jax.numpy as jnp
from jax import lax
from jax.experimental import pallas as pl
from jax.experimental.pallas import tpu as pltpu
from jax.sharding import PartitionSpec as P

PANEL = 256
WIDE = 2 * PANEL
LANE = 128
SUB = 8
P_CHUNKS = 6
HIGHEST = lax.Precision.HIGHEST
MESH = pl.DeviceIdType.MESH


def dot(a, b, ca=1, cb=0):
    return lax.dot_general(
        a, b, (((ca,), (cb,)), ((), ())), precision=HIGHEST, preferred_element_type=jnp.float32
    )


def row_chunks(rows, count):
    units = rows // SUB
    sizes = [units // count + (1 if i < units % count else 0) for i in range(count)]
    out, at = [], 0
    for size in sizes:
        if size:
            out.append((at * SUB, size * SUB))
            at += size
    return out


class AllReduce:
    def __init__(self, src, recv, dst, sems, n_row, me, col, count, base=0, height=None):
        self.src, self.recv, self.dst = src, recv, dst
        self.sems = sems
        self.n = n_row
        self.bits = n_row.bit_length() - 1
        self.col = col
        self.me = me
        self.chunks = []
        spin = max(self.bits - 1, 1)
        for c, (ro, rn) in enumerate(row_chunks(height or src.shape[1], count)):
            ro = pl.multiple_of(base + ro, SUB) if height else ro
            order = [(c + t) % spin for t in range(spin)] + list(range(spin, self.bits))
            starts = [0]
            mine = []
            for s, b in enumerate(order):
                bit = (me // (1 << b)) % 2
                mine.append(bit)
                starts.append(starts[-1] + bit * (n_row >> (s + 1)))
            self.chunks.append((c, ro, rn, order, starts, mine))

    def partner(self, b, bit):
        return self.me + (1 << b) * (1 - 2 * bit)

    def rs_copy(self, s, chunk):
        c, ro, rn, order, starts, mine = chunk
        half = self.n >> (s + 1)
        off = self.n - (self.n >> s)
        bit = mine[s]
        send = starts[s] + (1 - bit) * half
        return pltpu.make_async_remote_copy(
            src_ref=self.src.at[pl.ds(send, half), pl.ds(ro, rn), :],
            dst_ref=self.recv.at[pl.ds(off, half), pl.ds(ro, rn), :],
            send_sem=self.sems.at[0, s, c],
            recv_sem=self.sems.at[1, s, c],
            device_id=(self.partner(order[s], bit), self.col),
            device_id_type=MESH,
        )

    def rs_start(self, s):
        for chunk in self.chunks:
            self.rs_copy(s, chunk).start()

    def rs_finish(self, s, chunks):
        half = self.n >> (s + 1)
        off = self.n - (self.n >> s)
        last = s == self.bits - 1
        for chunk in chunks:
            c, ro, rn, order, starts, mine = chunk
            self.rs_copy(s, chunk).wait()
            keep = starts[s + 1]
            into = self.dst if last else self.src

            def add(i, carry, ro=ro, rn=rn, keep=keep, into=into):
                rows = pl.ds(ro, rn)
                into[keep + i, rows, :] = self.src[keep + i, rows, :] + self.recv[off + i, rows, :]
                return carry

            lax.fori_loop(0, half, add, 0)
            if not last:
                self.rs_copy(s + 1, chunk).start()
            else:
                self.ag_copy(s, chunk).start()

    def ag_copy(self, s, chunk):
        c, ro, rn, order, starts, mine = chunk
        half = self.n >> (s + 1)
        bit = mine[s]
        region = self.dst.at[pl.ds(starts[s + 1], half), pl.ds(ro, rn), :]
        return pltpu.make_async_remote_copy(
            src_ref=region,
            dst_ref=region,
            send_sem=self.sems.at[2, s, c],
            recv_sem=self.sems.at[3, s, c],
            device_id=(self.partner(order[s], bit), self.col),
            device_id_type=MESH,
        )

    def ag_finish(self, s, chunks):
        for chunk in chunks:
            self.ag_copy(s, chunk).wait()
            if s > 0:
                self.ag_copy(s - 1, chunk).start()

    def steps(self):
        groups = [self.chunks[i : i + 3] for i in range(0, len(self.chunks), 3)]
        out = []
        for s in range(self.bits):
            out += [functools.partial(self.rs_finish, s, group) for group in groups]
        for s in reversed(range(self.bits)):
            out += [functools.partial(self.ag_finish, s, group) for group in groups]
        return out


def split3(x):
    hi = x.astype(jnp.bfloat16).astype(jnp.float32)
    rest = x - hi
    mid = rest.astype(jnp.bfloat16).astype(jnp.float32)
    return hi, mid, rest - mid


def split2(x):
    hi = x.astype(jnp.bfloat16)
    return hi, (x - hi.astype(jnp.float32)).astype(jnp.bfloat16)


def dot3(a, b):
    def one(u, v):
        return jnp.dot(u, v, preferred_element_type=jnp.float32)

    return one(a[0], b[0]) + (one(a[0], b[1]) + one(a[1], b[0]))


def eliminate(x, lane, sub):
    d11 = d12 = d22 = None
    for a in range(0, SUB, 2):
        b = a + 1
        ca = jnp.broadcast_to(x[:, a : a + 1], x.shape)
        cb = jnp.broadcast_to(x[:, b : b + 1], x.shape)
        p11 = jnp.broadcast_to(ca[a : a + 1, :], x.shape)
        p12 = jnp.broadcast_to(cb[a : a + 1, :], x.shape)
        p22 = jnp.broadcast_to(cb[b : b + 1, :], x.shape)
        if a == 0:
            d11, d12, d22 = p11, p12, p22
        else:
            here = sub >= a
            d11 = jnp.where(here, p11, d11)
            d12 = jnp.where(here, p12, d12)
            d22 = jnp.where(here, p22, d22)
        if b == SUB - 1:
            break
        below = sub > b
        pair = (lane == a) | (lane == b)
        row_a = jnp.where(pair, jnp.where(lane == a, 1.0, 0.0), jnp.broadcast_to(x[a : a + 1, :], x.shape))
        row_b = jnp.where(pair, jnp.where(lane == b, 1.0, 0.0), jnp.broadcast_to(x[b : b + 1, :], x.shape))
        r = jnp.where(below, 1.0 / (p11 * p22 - p12 * p12), 0.0)
        num = (ca * p22 - cb * p12) * row_a + (cb * p11 - ca * p12) * row_b
        x = jnp.where(pair & below, 0.0, x) - num * r
    m = jnp.where(sub % 2 == 1, d12 / d11, 0.0)
    scale = lax.rsqrt(jnp.where(sub % 2 == 1, d22 - d12 * m, d11))
    y = jnp.where(lane == sub, 1.0, jnp.where(lane < sub - sub % 2, x, 0.0))
    return (y - m * pltpu.roll(y, 1, 0)) * scale


def factor_panels(t_ref, d_ref, k, lo, hi):
    base = k * LANE
    end = base + LANE
    size = t_ref.shape[0]
    lane = lax.broadcasted_iota(jnp.int32, (SUB, LANE), 1)
    sub = lax.broadcasted_iota(jnp.int32, (SUB, LANE), 0)
    full_lane = lax.broadcasted_iota(jnp.int32, (LANE, LANE), 1)
    full_sub = lax.broadcasted_iota(jnp.int32, (LANE, LANE), 0)
    if lo == 0:
        d_ref[...] = t_ref[base:end, base:end]

    def one(p, carry):
        r0 = pl.multiple_of(p * SUB, SUB)
        pan = d_ref[pl.ds(r0, SUB), :]
        inv = eliminate(pltpu.roll(pan, (LANE - r0) % LANE, 1), lane, sub)
        rel = lane - r0
        inside = (rel >= 0) & (rel < SUB)
        pan = jnp.where(inside, jnp.where(rel == sub, 1.0, 0.0), pan)
        terms = [inv[:, j : j + 1] * pan[j : j + 1, :] for j in range(SUB)]
        while len(terms) > 1:
            terms = [terms[i] + terms[i + 1] for i in range(0, len(terms), 2)]
        top = terms[0]
        m1, m2, m3 = split3(top)
        after = rel >= SUB
        w1, w2, w3 = (jnp.where(after, v, 0.0) for v in (m1, m2, m3))
        left = jnp.concatenate([w1, w1, w2, w1, w2, w3], axis=0).astype(jnp.bfloat16)
        right = jnp.concatenate([m1, m2, m1, m3, m2, m1], axis=0).astype(jnp.bfloat16)
        upd = lax.dot_general(
            left, right, (((0,), (0,)), ((), ())), preferred_element_type=jnp.float32
        )
        clear = (full_lane >= r0) & (full_lane < r0 + SUB)
        d_ref[...] = jnp.where(clear, 0.0, d_ref[...]) - upd
        d_ref[pl.ds(r0, SUB), :] = top
        return carry

    lax.fori_loop(lo, hi, one, 0)
    if hi * SUB == LANE:
        inv = jnp.where(full_lane <= full_sub, d_ref[...], 0.0)
        for c in range(size // LANE):
            at = slice(c * LANE, (c + 1) * LANE)
            if c != k:
                t_ref[base:end, at] = dot(inv, t_ref[base:end, at])
        t_ref[base:end, base:end] = inv
        if end < size:
            t_ref[end:, base:end] = jnp.zeros((size - end, LANE), jnp.float32)
            low = t_ref[base:end, end:].T
            t_ref[end:, :] = t_ref[end:, :] - dot(low, t_ref[base:end, :])


def kernel(n_row, n_col, scale, a_ref, top_ref, basis_ref, a12, a12t, p, p_in, q, g, g_in, gq, t, d,
           p_sems, g_sems, bsend, brecv, xsend, xrecv):
    me = lax.axis_index("row")
    col = lax.axis_index("col")
    bits = n_row.bit_length() - 1
    blocks = a_ref.shape[1] // LANE
    gblocks = WIDE // LANE
    p_split = p.shape[0] // blocks
    g_split = g.shape[0] // gblocks

    barrier = pltpu.get_barrier_semaphore()
    for b in range(bits):
        bit = (me // (1 << b)) % 2
        pl.semaphore_signal(
            barrier, inc=1, device_id=(me + (1 << b) * (1 - 2 * bit), col), device_id_type=MESH
        )
    for c in range(1, n_col):
        pl.semaphore_signal(barrier, inc=1, device_id=(me, (col + c) % n_col), device_id_type=MESH)
    pl.semaphore_wait(barrier, bits + n_col - 1)

    def panel_copy(c):
        return pltpu.make_async_remote_copy(
            src_ref=a_ref.at[:, pl.ds(0, WIDE)],
            dst_ref=a12,
            send_sem=bsend.at[c],
            recv_sem=brecv.at[0],
            device_id=(me, c),
            device_id_type=MESH,
        )

    @pl.when(col == 0)
    def _():
        for c in range(1, n_col):
            panel_copy(c).start()
        a12[...] = a_ref[:, :WIDE]
        for c in range(1, n_col):
            panel_copy(c).wait_send()

    @pl.when(col != 0)
    def _():
        panel_copy(0).wait_recv()

    a12t[...] = a12[...].T

    def fill(dst, src, split, exact):
        pair = 2 * LANE
        left = a12t[...] if exact else split2(a12t[...])

        def one(i, carry):
            cols = src[:, pl.ds(pl.multiple_of(i * pair, pair), pair)]
            val = dot(left, cols) if exact else dot3(left, split2(cols))
            for h in range(2):
                part = val[:, h * LANE : (h + 1) * LANE]
                dst[pl.ds((2 * i + h) * split, split)] = part.reshape(split, WIDE // split, LANE)
            return carry

        lax.fori_loop(0, src.shape[1] // pair, one, 0)

    fill(g, a12, g_split, True)
    shared = (g.shape[1] // SUB) % n_col == 0 and n_col > 1
    g_high = g.shape[1] // n_col if shared else None
    g_base = col * g_high if shared else 0
    g_red = AllReduce(g, g_in, gq, g_sems, n_row, me, col, 3, g_base, g_high)
    g_red.rs_start(0)
    fill(p, a_ref, p_split, False)
    for step in g_red.steps():
        step()
    if shared:
        part = gq.at[:, pl.ds(pl.multiple_of(g_base, SUB), g_high), :]
        swaps = [
            pltpu.make_async_remote_copy(
                src_ref=part,
                dst_ref=part,
                send_sem=xsend.at[c],
                recv_sem=xrecv.at[c],
                device_id=(me, (col + c) % n_col),
                device_id_type=MESH,
            )
            for c in range(1, n_col)
        ]
        for swap in swaps:
            swap.start()
    p_red = AllReduce(p, p_in, q, p_sems, n_row, me, col, P_CHUNKS)
    p_red.rs_start(0)
    if shared:
        for swap in swaps:
            swap.wait()
    for b in range(gblocks):
        t[:, b * LANE : (b + 1) * LANE] = gq[b * g_split : (b + 1) * g_split].reshape(WIDE, LANE)

    rows = lax.broadcasted_iota(jnp.int32, (WIDE, WIDE), 0)
    cols = lax.broadcasted_iota(jnp.int32, (WIDE, WIDE), 1)
    diag = jnp.where(cols == rows, t[...], 0.0)
    norm = lax.rsqrt(jnp.sum(diag, axis=0, keepdims=True))
    t[...] = t[...] * lax.rsqrt(jnp.sum(diag, axis=1, keepdims=True)) * norm

    per = LANE // SUB
    few = per // 4
    units = [(k, lo, lo + few) for k in range(gblocks) for lo in range(0, per, few)]
    steps = p_red.steps()
    done = 0
    for i, step in enumerate(steps):
        upto = min(len(units) * (i + 1) // (len(steps) - 2), len(units))
        for unit in units[done:upto]:
            factor_panels(t, d, *unit)
        done = upto
        if i == len(steps) - 2:
            t[...] = jnp.where(cols <= rows, t[...] * norm, 0.0)
            basis_ref[...] = dot(a12[...], t[...], 1, 1) * scale
        step()


    inverse = split2(t[...])

    def finish(i, carry):
        pair = 2 * LANE
        parts = [
            q[pl.ds((2 * i + h) * p_split, p_split)].reshape(WIDE, LANE) for h in range(2)
        ]
        val = dot3(inverse, split2(jnp.concatenate(parts, axis=1)))
        r = lax.broadcasted_iota(jnp.int32, (WIDE, pair), 0)
        c = lax.broadcasted_iota(jnp.int32, (WIDE, pair), 1) + col * a_ref.shape[1] + i * pair
        top_ref[:, pl.ds(pl.multiple_of(i * pair, pair), pair)] = jnp.where(c >= r, val, 0.0)
        return carry

    lax.fori_loop(0, blocks // 2, finish, 0)


def body(n_row, n_col, matrix):
    height, width = matrix.shape
    scale = math.sqrt(height * n_row)
    bits = n_row.bit_length() - 1
    p_shape = (n_row, (width // LANE) * WIDE // n_row, LANE)
    g_shape = (n_row, (WIDE // LANE) * WIDE // n_row, LANE)
    f32 = jnp.float32
    vmem = pl.BlockSpec(memory_space=pltpu.VMEM)
    return pl.pallas_call(
        functools.partial(kernel, n_row, n_col, scale),
        out_shape=(
            jax.ShapeDtypeStruct((WIDE, width), f32),
            jax.ShapeDtypeStruct((height, WIDE), f32),
        ),
        in_specs=[vmem],
        out_specs=(vmem, vmem),
        scratch_shapes=[
            pltpu.VMEM((height, WIDE), f32),
            pltpu.VMEM((WIDE, height), f32),
            pltpu.VMEM(p_shape, f32),
            pltpu.VMEM(p_shape, f32),
            pltpu.VMEM(p_shape, f32),
            pltpu.VMEM(g_shape, f32),
            pltpu.VMEM(g_shape, f32),
            pltpu.VMEM(g_shape, f32),
            pltpu.VMEM((WIDE, WIDE), f32),
            pltpu.VMEM((LANE, LANE), f32),
            pltpu.SemaphoreType.DMA((4, bits, P_CHUNKS)),
            pltpu.SemaphoreType.DMA((4, bits, 3)),
            pltpu.SemaphoreType.DMA((n_col,)),
            pltpu.SemaphoreType.DMA((1,)),
            pltpu.SemaphoreType.DMA((n_col,)),
            pltpu.SemaphoreType.DMA((n_col,)),
        ],
        compiler_params=pltpu.CompilerParams(
            collective_id=0, has_side_effects=True, vmem_limit_bytes=60 * 1024 * 1024
        ),
    )(matrix)


def solution(mesh):
    return jax.shard_map(
        functools.partial(body, mesh.shape["row"], mesh.shape["col"]),
        mesh=mesh,
        in_specs=(P("row", "col"),),
        out_specs=(P(None, "col"), P("row", None)),
        check_vma=False,
    )
```
